1024 devices in a mesh: ctx: 128 (over y, z), head: 8 (over x, core).
Axes of the slice: x: 4, y: 4, z: 32, core: 2. Of those that a mesh axis runs over, the one named last changes fastest.
Arguments:
- queries: bfloat16 [32768, 6144], P(('ctx', 'head')), may hold values from -120 to 120
- keys: bfloat16 [32768, 1024], P(('ctx', 'head')), may hold values from -6 to 6
- values: bfloat16 [32768, 1024], P(('ctx', 'head')), may hold values from -6 to 6
- outputs: bfloat16 [32768, 6144], P(('ctx', 'head')), may hold values from -6 to 6
- out_grad: bfloat16 [32768, 6144], P(('ctx', 'head')), may hold values from -6 to 6
- frame_lists: int32 [128, 5], P('ctx'), may hold values from -1 to 127, as said below
Outputs:
- grad_queries: bfloat16 [32768, 6144], P('ctx', 'head')
- key_gradient: bfloat16 [32768, 1024], P('ctx', 'head')
- value_gradient: bfloat16 [32768, 1024], P('ctx', 'head')
The draws below stay inside these ranges and needn't reach their ends.
Inputs may be any that keep to these rules, and one draw needn't show every extreme that they name: `frame_lists`: entry o of the list of query frame f is f - o or -1 (always -1 where f - o < 0); entry 0 is f; entry 4 is f - 4 for every frame f divisible by 3 with f >= 4.
All inputs are finite; a program needn't handle non-finite values.
Results may differ from the reference program's by a relative error of at most 0.005.
Values may be sent and summed in bfloat16 or wider, within the bound.
No kernel may reach another device: no remote copies, remote signals or barrier semaphores. Data moves between devices by JAX's collectives and lax.ppermute only.
A program may use at most 32 MiB of HBM per device.

```python
import jax
import jax.numpy as jnp
from jax import lax

QUERY_HEAD_COUNT = 48
KEY_VALUE_HEADS = 8
HEAD_SIZE = 128
TOK_DEV = 256
FRAME = 256
REACH = 4
SEQUENCE_TOKENS = 32768
FRAMES = 128
LIST = 5
N_CTX = 128


def attention_pair(key):
    base = jax.random.fold_in(key, 11)
    key_query, key_random_seed = jax.random.split(base, 2)
    query_draw = jnp.clip(jax.random.normal(key_query, (SEQUENCE_TOKENS, QUERY_HEAD_COUNT * HEAD_SIZE), jnp.float32), -6.0, 6.0)
    key_sample = jnp.clip(jax.random.normal(key_random_seed, (SEQUENCE_TOKENS, KEY_VALUE_HEADS * HEAD_SIZE), jnp.float32), -6.0, 6.0)
    return (query_draw, key_sample)


def draw_queries(key, part):
    return attention_pair(key)[0].astype(jnp.bfloat16)


def draw_keys(key, part):
    return attention_pair(key)[1].astype(jnp.bfloat16)


def draw_frame_lists(key, part):
    frame_pos = jnp.arange(FRAMES, dtype=jnp.int32)[:, None]
    offset = jnp.arange(LIST, dtype=jnp.int32)[None, :]
    coin = jax.random.randint(jax.random.fold_in(key, 23), (FRAMES, LIST), 0, 2)
    keep = (coin == 1) | (offset == 0) | (offset == LIST - 1) & (frame_pos % 3 == 0)
    return jnp.where(keep & (frame_pos - offset >= 0), frame_pos - offset, -1).astype(jnp.int32)


def steps_of(rng, dims, pieces, low, high):
    loudness = 1.0
    for position, blocks in pieces:
        heights = jax.random.uniform(jax.random.fold_in(jax.random.fold_in(rng, 6), position), (blocks,), jnp.float32, low / len(pieces), high / len(pieces))
        loudness = loudness * jnp.repeat(jnp.exp(heights), dims[position] // blocks).reshape((-1,) + (1,) * (len(dims) - 1 - position))
    return loudness


def noise(stream_key, extent, spread, most, shards=(), held_as=jnp.bfloat16):
    entries = jax.random.normal(stream_key, extent, jnp.float32) * spread
    if len(shards) > 0:
        entries = steps_of(stream_key, extent, shards, -0.22, 0.18) * entries
    return jnp.clip(entries, min=-most, max=most).astype(held_as)


def setup_inputs(seed: int = 0) -> dict:
    key_of = jax.random.split(jax.random.key(seed), 7)
    return {
        "queries": draw_queries(jax.random.fold_in(key_of[6], 71), 0),
        "keys": draw_keys(jax.random.fold_in(key_of[6], 71), 0),
        "values": noise(key_of[2], (SEQUENCE_TOKENS, KEY_VALUE_HEADS * HEAD_SIZE), 1.0, 6.0, ((0, 1024),)),
        "outputs": noise(key_of[3], (SEQUENCE_TOKENS, QUERY_HEAD_COUNT * HEAD_SIZE), 1.0, 6.0, ((0, 1024),)),
        "out_grad": noise(key_of[4], (SEQUENCE_TOKENS, QUERY_HEAD_COUNT * HEAD_SIZE), 1.0, 6.0, ((0, 1024),)),
        "frame_lists": draw_frame_lists(jax.random.fold_in(key_of[6], 71), 0),
    }


def reference(queries, keys, values, outputs, out_grad, frame_lists):
    score_scaling = HEAD_SIZE ** -0.5
    frame_window = REACH * TOK_DEV
    query_group_width = QUERY_HEAD_COUNT // KEY_VALUE_HEADS
    frames_dev = TOK_DEV // FRAME
    key_extent = frame_window + TOK_DEV
    key_padding = jnp.concatenate([jnp.zeros((frame_window, KEY_VALUE_HEADS * HEAD_SIZE), keys.dtype), keys], axis=0)
    value_padding = jnp.concatenate([jnp.zeros((frame_window, KEY_VALUE_HEADS * HEAD_SIZE), values.dtype), values], axis=0)
    row_delta = jnp.sum((out_grad.astype(jnp.float32) * outputs.astype(jnp.float32)).reshape(SEQUENCE_TOKENS, QUERY_HEAD_COUNT, HEAD_SIZE), axis=2)

    def block(carry, block_index):
        key_gradient, value_gradient = carry
        start_position = (block_index * TOK_DEV).astype(jnp.int32)
        query_block_rows = lax.dynamic_slice_in_dim(queries, start_position, TOK_DEV, 0).reshape(TOK_DEV, QUERY_HEAD_COUNT, HEAD_SIZE).astype(jnp.float32)
        gradient_block = lax.dynamic_slice_in_dim(out_grad, start_position, TOK_DEV, 0).reshape(TOK_DEV, QUERY_HEAD_COUNT, HEAD_SIZE).astype(jnp.float32)
        delta_blk = lax.dynamic_slice_in_dim(row_delta, start_position, TOK_DEV, 0)
        key_block_rows = lax.dynamic_slice_in_dim(key_padding, start_position, key_extent, 0).reshape(key_extent, KEY_VALUE_HEADS, HEAD_SIZE).astype(jnp.float32)
        value_block_rows = lax.dynamic_slice_in_dim(value_padding, start_position, key_extent, 0).reshape(key_extent, KEY_VALUE_HEADS, HEAD_SIZE).astype(jnp.float32)
        key_wide = jnp.repeat(key_block_rows, query_group_width, axis=1)
        value_wide = jnp.repeat(value_block_rows, query_group_width, axis=1)
        lists = lax.dynamic_slice_in_dim(frame_lists, (block_index * frames_dev).astype(jnp.int32), frames_dev, 0)
        key_tok = start_position - frame_window + jnp.arange(key_extent, dtype=jnp.int32)
        key_frame = jnp.floor_divide(key_tok, FRAME)
        listed = jnp.any(lists[:, :, None] == key_frame[None, None, :], axis=1) & (key_tok >= 0)[None, :]
        allowed = jnp.repeat(listed, FRAME, axis=0)
        scores = jnp.einsum('thd,lhd->htl', query_block_rows, key_wide) * score_scaling
        scores = jnp.where(allowed[None], scores, -jnp.inf)
        peak = jnp.max(scores, axis=2, keepdims=True)
        lse = peak + jnp.log(jnp.sum(jnp.exp(scores - peak), axis=2, keepdims=True))
        probs = jnp.exp(scores - lse)
        probability_block = lax.optimization_barrier(probs.astype(jnp.bfloat16)).astype(jnp.float32)
        dprobs = jnp.einsum('thd,lhd->htl', gradient_block, value_wide)
        dscores = probs * (dprobs - delta_blk.T[:, :, None])
        score_gradient_block = lax.optimization_barrier(dscores.astype(jnp.bfloat16)).astype(jnp.float32)
        grad_q = (jnp.einsum('htl,lhd->thd', score_gradient_block, key_wide) * score_scaling).astype(jnp.bfloat16)
        key_gradient_terms = jnp.einsum('yzk,zyq->kyq', score_gradient_block, query_block_rows).reshape(key_extent, KEY_VALUE_HEADS, query_group_width, HEAD_SIZE).sum(axis=2) * score_scaling
        value_gradient_terms = jnp.einsum('yzk,zyq->kyq', probability_block, gradient_block).reshape(key_extent, KEY_VALUE_HEADS, query_group_width, HEAD_SIZE).sum(axis=2)
        earlier_keys = lax.dynamic_slice_in_dim(key_gradient, start_position, key_extent, 0)
        earlier_values = lax.dynamic_slice_in_dim(value_gradient, start_position, key_extent, 0)
        key_gradient = lax.dynamic_update_slice_in_dim(key_gradient, earlier_keys + key_gradient_terms.reshape(key_extent, KEY_VALUE_HEADS * HEAD_SIZE), start_position, 0)
        value_gradient = lax.dynamic_update_slice_in_dim(value_gradient, earlier_values + value_gradient_terms.reshape(key_extent, KEY_VALUE_HEADS * HEAD_SIZE), start_position, 0)
        return (key_gradient, value_gradient), grad_q.reshape(TOK_DEV, QUERY_HEAD_COUNT * HEAD_SIZE)

    empty_block = jnp.zeros((frame_window + SEQUENCE_TOKENS, KEY_VALUE_HEADS * HEAD_SIZE), jnp.float32)
    (key_gradient, value_gradient), grad_blocks = lax.scan(block, (empty_block, empty_block), jnp.arange(N_CTX, dtype=jnp.int32))
    grad_queries = grad_blocks.reshape(SEQUENCE_TOKENS, QUERY_HEAD_COUNT * HEAD_SIZE)
    return grad_queries, key_gradient[frame_window:].astype(jnp.bfloat16), value_gradient[frame_window:].astype(jnp.bfloat16)
```

```python
import functools

import jax
import jax.numpy as jnp
from jax import lax
from jax.experimental import pallas as pl
from jax.experimental.pallas import tpu as pltpu
from jax.sharding import PartitionSpec as P

HEAD = 128
GROUP = 6
KV_HEADS = 8
TOK = 256
ROWS = 32
REACH = 4
SCALE = HEAD ** (-0.5)
QG = 2 * GROUP * HEAD
WIDE = QG + HEAD
F32 = jnp.float32
BF16 = jnp.bfloat16
VMEM = pl.BlockSpec(memory_space=pltpu.VMEM)
SMEM = pl.BlockSpec(memory_space=pltpu.SMEM)


def shifted(value, steps):
    count = lax.axis_size("ctx")
    first, last = max(0, -steps), min(count, count - steps)
    return lax.ppermute(value, "ctx", [(s, s + steps) for s in range(first, last)])


def regroup(value):
    return lax.all_to_all(value, "head", split_axis=0, concat_axis=0, tiled=True)


def pack_kv_kernel(k_ref, v_ref, out_ref):
    for h in range(KV_HEADS):
        out_ref[h, :, :HEAD] = k_ref[:, h * HEAD : (h + 1) * HEAD]
        out_ref[h, :, HEAD:] = v_ref[:, h * HEAD : (h + 1) * HEAD]


def pack_qg_kernel(q_ref, g_ref, o_ref, out_ref):
    lane = lax.broadcasted_iota(jnp.int32, (ROWS, HEAD), 1)
    width = GROUP * HEAD
    for h in range(KV_HEADS):
        out_ref[h, :, :width] = q_ref[:, h * width : (h + 1) * width]
        out_ref[h, :, width:QG] = g_ref[:, h * width : (h + 1) * width]
        delta = jnp.zeros((ROWS, HEAD), F32)
        for i in range(GROUP):
            cols = slice(h * width + i * HEAD, h * width + (i + 1) * HEAD)
            term = jnp.sum(g_ref[:, cols].astype(F32) * o_ref[:, cols].astype(F32), axis=1, keepdims=True)
            delta = jnp.where(jnp.bitwise_and(lane, 7) == i, term, delta)
        high = delta.astype(BF16).astype(F32)
        rest = delta - high
        middle = rest.astype(BF16).astype(F32)
        low = rest - middle
        mixed = jnp.where(lane < 8, high, jnp.where(lane < 16, middle, low))
        out_ref[h, :, QG:] = mixed.astype(BF16)


def dot(a, b, dims):
    return lax.dot_general(a, b, (dims, ((), ())), preferred_element_type=F32)


NT = ((1,), (1,))
NN = ((1,), (0,))


def attention_kernel(
    lists_ref, qg_ref, kv0_ref, kv13_ref, kv2_ref, kv4_ref,
    dq_ref, send_ref, keep_ref, own_ref,
    delta_ref, kt_ref, acc_ref,
):
    def kv(o):
        return {
            0: kv0_ref, 1: kv13_ref.at[:TOK], 2: kv2_ref, 3: kv13_ref.at[TOK:], 4: kv4_ref,
        }[o]

    offsets = range(REACH + 1)
    for o in offsets:
        kt_ref[:, o * TOK : (o + 1) * TOK] = kv(o)[:, :HEAD].T
    packed = qg_ref[:, QG:].astype(F32).T
    delta_ref[...] = packed[0:8] + packed[8:16] + packed[16:24]
    acc_ref[...] = jnp.zeros_like(acc_ref)
    listed = [lists_ref[0, o] >= 0 for o in offsets]

    def head(i, carry):
        q = qg_ref[:, pl.ds(pl.multiple_of(i * HEAD, HEAD), HEAD)]
        g = qg_ref[:, pl.ds(pl.multiple_of((GROUP + i) * HEAD, HEAD), HEAD)]
        delta = delta_ref[pl.ds(i, 1), :]
        scores = [dot(kv(o)[:, :HEAD], q, NT) for o in offsets]
        peak = jnp.full((1, TOK), -jnp.inf, F32)
        for o in offsets:
            top = jnp.max(scores[o], axis=0, keepdims=True)
            peak = jnp.maximum(peak, jnp.where(listed[o], top, -jnp.inf))
        weights, total = [], jnp.zeros((1, TOK), F32)
        for o in offsets:
            bound = jnp.where(listed[o], peak, jnp.inf)
            w = jnp.exp((scores[o] - bound) * SCALE)
            weights.append(w)
            total = total + jnp.sum(w, axis=0, keepdims=True)
        inverse = 1.0 / total
        dqt = jnp.zeros((HEAD, TOK), F32)
        for o in offsets:
            probs = weights[o] * inverse
            dprobs = dot(kv(o)[:, HEAD:], g, NT)
            ds = (probs * (dprobs - delta)).astype(BF16)
            acc_ref[o, :, :HEAD] += dot(ds, q, NN)
            acc_ref[o, :, HEAD:] += dot(probs.astype(BF16), g, NN)
            dqt = dqt + dot(kt_ref[:, o * TOK : (o + 1) * TOK], ds, NN)
        dq_ref[:, pl.ds(pl.multiple_of(i * HEAD, HEAD), HEAD)] = (dqt * SCALE).T.astype(BF16)
        return carry

    lax.fori_loop(0, GROUP, head, 0)
    scale = jnp.where(lax.broadcasted_iota(jnp.int32, (1, 2 * HEAD), 1) < HEAD, SCALE, 1.0)
    send_ref[:TOK] = (acc_ref[4] * scale).astype(BF16)
    send_ref[TOK:] = (acc_ref[2] * scale).astype(BF16)
    keep_ref[:TOK] = acc_ref[3] * scale
    keep_ref[TOK:] = acc_ref[1] * scale
    own_ref[...] = acc_ref[0] * scale


def on_device(queries, keys, values, outputs, out_grad, frame_lists):
    kv_packed = pl.pallas_call(
        pack_kv_kernel,
        out_shape=jax.ShapeDtypeStruct((KV_HEADS, ROWS, 2 * HEAD), BF16),
        in_specs=[VMEM] * 2,
        out_specs=VMEM,
        compiler_params=pltpu.CompilerParams(vmem_limit_bytes=2 << 20),
        name="pack_kv",
    )(keys, values)
    qg_packed = pl.pallas_call(
        pack_qg_kernel,
        out_shape=jax.ShapeDtypeStruct((KV_HEADS, ROWS, WIDE), BF16),
        in_specs=[VMEM] * 3,
        out_specs=VMEM,
        cost_estimate=pl.CostEstimate(flops=1_000_000, bytes_accessed=3_000_000, transcendentals=0),
        compiler_params=pltpu.CompilerParams(vmem_limit_bytes=6 << 20),
        name="pack_qg",
    )(queries, out_grad, outputs)
    kv0 = regroup(kv_packed).reshape(TOK, 2 * HEAD)
    qg = regroup(qg_packed).reshape(TOK, WIDE)
    kv2 = shifted(kv0, 2)
    kv13 = shifted(jnp.concatenate([kv0, kv2], axis=0), 1)
    kv4 = shifted(kv2, 2)
    width = 2 * HEAD
    dq, send, keep, own = pl.pallas_call(
        attention_kernel,
        out_shape=(
            jax.ShapeDtypeStruct((TOK, GROUP * HEAD), BF16),
            jax.ShapeDtypeStruct((2 * TOK, width), BF16),
            jax.ShapeDtypeStruct((2 * TOK, width), F32),
            jax.ShapeDtypeStruct((TOK, width), F32),
        ),
        in_specs=[SMEM] + [VMEM] * 5,
        out_specs=(VMEM,) * 4,
        scratch_shapes=[
            pltpu.VMEM((8, TOK), F32),
            pltpu.VMEM((HEAD, (REACH + 1) * TOK), BF16),
            pltpu.VMEM((REACH + 1, TOK, width), F32),
        ],
        cost_estimate=pl.CostEstimate(flops=2_600_000_000, bytes_accessed=4_000_000, transcendentals=2_000_000),
        compiler_params=pltpu.CompilerParams(vmem_limit_bytes=24 << 20),
        name="attention",
    )(frame_lists, qg, kv0, kv13, kv2, kv4)
    came = shifted(send, -1).astype(F32) + keep
    came = came.astype(BF16)
    far = shifted(came[:TOK], -3)
    near = shifted(came[TOK:], -1)
    total = own + far.astype(F32) + near.astype(F32)
    return dq, total[:, :HEAD].astype(BF16), total[:, HEAD:].astype(BF16)


def solution(mesh):
    both = P(("ctx", "head"), None)
    return jax.shard_map(
        on_device,
        mesh=mesh,
        in_specs=(both,) * 5 + (P("ctx", None),),
        out_specs=(P("ctx", "head"),) * 3,
        check_vma=False,
    )
```
